128 devices in a mesh: ctx: 32 (over x_lo, y, z), fft: 4 (over x_hi, core).
Axes of the slice: x: 4 (x_hi: 2, x_lo: 2; x = x_hi * 2 + x_lo), y: 4, z: 4, core: 2. Of those that a mesh axis runs over, the one named last changes fastest.
Arguments:
- qkv: bfloat16 [16384, 3, 4096], P('ctx', None, 'fft'), may hold values from -6 to 6
- short_w: bfloat16 [3, 3, 4096], P(None, None, 'fft'), may hold values from -3.5 to 3.5
- skip: float32 [4096], P('fft'), may hold values from -4 to 4
- long_h: float32 [4, 32, 2, 16384], P(None, 'ctx'), may hold values from -1 to 1
Outputs:
- hyena_out: bfloat16 [16384, 4096], P('ctx', 'fft')
The draws below stay inside these ranges and needn't reach their ends.
All inputs are finite; a program needn't handle non-finite values.
Results may differ from the reference program's by a relative error of at most 0.0075.
Values may be sent and summed in bfloat16 or wider, within the bound.
No kernel may reach another device: no remote copies, remote signals or barrier semaphores. Data moves between devices by JAX's collectives and lax.ppermute only.
A program may use at most 128 MiB of HBM per device.

```python
import math
import jax
import jax.numpy as jnp
from jax import lax

D = 4096
GROUP = 16
K_SHORT = 3
STRAND_SYMBOLS = 16384
KERNEL_CLUSTERS = 256
CG = 2
N_CTX = 32
N_FFT = 4


def draw_long_h(key, part):
    seed_jitter = jax.random.fold_in(key, 0)
    seed_extent = jax.random.fold_in(key, 1)
    seed_spike = jax.random.fold_in(key, 4)
    seed_multiplier = jax.random.fold_in(key, 5)
    symbol_lag = jnp.arange(STRAND_SYMBOLS, dtype=jnp.float32)[None, :]
    decay_len = jnp.exp(jax.random.uniform(seed_extent, (KERNEL_CLUSTERS, 1), jnp.float32, math.log(30.0), math.log(4.0 * STRAND_SYMBOLS)))
    noise = jnp.clip(jax.random.normal(seed_jitter, (KERNEL_CLUSTERS, STRAND_SYMBOLS), jnp.float32), -4.0, 4.0)
    rate = 1.0 / decay_len
    amplitude = jnp.sqrt(1.0 - jnp.exp(-2.0 * rate))
    spike_location = jax.random.uniform(seed_spike, (KERNEL_CLUSTERS, 3), jnp.float32, 1.0, float(STRAND_SYMBOLS))
    kernel_multipliers = jax.random.uniform(seed_multiplier, (KERNEL_CLUSTERS, 3), jnp.float32, 0.5, 0.8)
    fading_profile = amplitude * jnp.exp(-rate * symbol_lag)
    for symbol_ordinal in range(3):
        fading_profile = fading_profile * jnp.where(symbol_lag >= spike_location[:, symbol_ordinal:symbol_ordinal + 1], kernel_multipliers[:, symbol_ordinal:symbol_ordinal + 1], 1.0)
    taps = jnp.clip(fading_profile * noise, -1.0, 1.0)
    return taps.reshape(N_FFT, N_CTX, CG, STRAND_SYMBOLS).astype(jnp.float32)


def block_levels(own_key, shape, cuts, least, largest):
    loudness, own = 1.0, jax.random.fold_in(own_key, 6)
    for position, blocks in cuts:
        heights = jnp.exp(jax.random.uniform(jax.random.fold_in(own, position), (blocks,), jnp.float32, least / len(cuts), largest / len(cuts)))
        loudness = loudness * jnp.repeat(heights, shape[position] // blocks).reshape([-1 if axis == position else 1 for axis in range(len(shape))])
    return loudness


def gaussian(stream_key, dims, width, bound, cuts=(), held_as=jnp.bfloat16):
    level = block_levels(stream_key, dims, cuts, -0.22, 0.18) if cuts else 1.0
    drawn = jax.random.normal(stream_key, dims, jnp.float32) * width * level
    return jnp.minimum(jnp.maximum(drawn, -bound), bound).astype(held_as)


def setup_inputs(seed: int = 0) -> dict:
    key_of = jax.random.split(jax.random.key(seed), 5)
    qkv = gaussian(key_of[0], (STRAND_SYMBOLS, 3, D), 1.0, 6.0, ((0, 32), (2, 4)))
    short_w = gaussian(key_of[1], (K_SHORT, 3, D), K_SHORT ** -0.5, 3.5, ((2, 4),))
    skip = gaussian(key_of[2], (D,), 1.0, 4.0, ((0, 4),), jnp.float32)
    long_h = draw_long_h(jax.random.fold_in(key_of[4], 71), 0)
    return dict(qkv=qkv, short_w=short_w, skip=skip, long_h=long_h)


def causal_depthwise(signal, kernel):
    taps = kernel.shape[0]
    rows = signal.shape[0]
    padded = jnp.concatenate([jnp.zeros((taps - 1, signal.shape[1]), jnp.float32), signal.astype(jnp.float32)], axis=0)
    kernel_wide = kernel.astype(jnp.float32)
    total = kernel_wide[0][None, :] * padded[taps - 1:taps - 1 + rows]
    for offset in range(1, taps):
        total = total + kernel_wide[offset][None, :] * padded[taps - 1 - offset:taps - 1 - offset + rows]
    return total


def group_conv(operands):
    block, spectrum = operands
    length = block.shape[1]
    product = jnp.fft.rfft(block, n=2 * length) * spectrum[None, :]
    return jnp.fft.irfft(product, n=2 * length)[:, :length]


def reference(qkv, short_w, skip, long_h):
    feat = causal_depthwise(qkv.reshape(STRAND_SYMBOLS, 3 * D), short_w.reshape(K_SHORT, 3 * D))
    gated = (feat[:, D:2 * D] * feat[:, 2 * D:]).astype(jnp.bfloat16)
    taps = long_h.reshape(KERNEL_CLUSTERS, STRAND_SYMBOLS)
    spectra = jnp.fft.rfft(taps, n=2 * STRAND_SYMBOLS)
    columns = gated.astype(jnp.float32).T.reshape(KERNEL_CLUSTERS, GROUP, STRAND_SYMBOLS)
    result = lax.map(group_conv, (columns, spectra))
    longconv = result.reshape(D, STRAND_SYMBOLS).T.astype(jnp.bfloat16)
    inner = longconv.astype(jnp.float32) + skip[None, :] * gated.astype(jnp.float32)
    return (feat[:, :D] * inner).astype(jnp.bfloat16)
```

```python
import functools

import jax
import jax.numpy as jnp
from jax import lax
from jax.experimental import pallas as pl
from jax.experimental.pallas import tpu as pltpu
from jax.sharding import PartitionSpec as P

GROUP = 16
LANES = 256
SUB = 256


def depthwise(rows_ref, halo, taps, scratch):
    rows = rows_ref.shape[0]
    scratch[8:, :] = rows_ref[...].astype(jnp.float32)
    scratch[8 - halo.shape[0] : 8, :] = halo
    total = taps[0:1, :] * scratch[8 : 8 + rows, :]
    for offset in range(1, taps.shape[0]):
        total = total + taps[offset : offset + 1, :] * scratch[8 - offset : 8 - offset + rows, :]
    return total


def gate_kernel(streams_ref, halo_ref, taps_ref, gated_ref, turned_ref, first, second):
    taps = taps_ref[...].astype(jnp.float32)
    halo = halo_ref[...].astype(jnp.float32)
    feat_one = depthwise(streams_ref.at[0], halo[1], taps[1], first)
    feat_two = depthwise(streams_ref.at[1], halo[2], taps[2], second)
    gated = (feat_one * feat_two).astype(jnp.bfloat16)
    gated_ref[...] = gated
    turned_ref[...] = gated.T


def finish_kernel(stream_ref, halo_ref, taps_ref, skip_ref, gated_ref, back_ref, out_ref, scratch):
    taps = taps_ref[0].astype(jnp.float32)
    query = depthwise(stream_ref.at[0], halo_ref[0].astype(jnp.float32), taps, scratch)
    inner = back_ref[...].T.astype(jnp.float32) + skip_ref[...] * gated_ref[...].astype(jnp.float32)
    out_ref[...] = (query * inner).astype(jnp.bfloat16)


def conv_kernel(signal_ref, taps_ref, out_ref, table, total):
    chunks, group, width = signal_ref.shape
    span = taps_ref.shape[-1]
    step = 1024
    for start in range(0, span - SUB, step):
        size = min(step, span - SUB - start)
        window = jnp.broadcast_to(taps_ref[0, :, start : start + size + SUB], (SUB, size + SUB))
        turned = pltpu.roll(window, 0, axis=1, stride=1, stride_axis=0)
        table[:, start : start + size] = turned[:, SUB:].astype(jnp.bfloat16)
    signal = signal_ref[...].reshape(chunks * group, width)
    for lag in range(chunks):
        rows = (chunks - lag) * group
        at = lag * width + SUB
        weights = jnp.concatenate(
            [table[:, at - half * SUB : at - half * SUB + width] for half in range(width // SUB)],
            axis=0,
        )
        part = jnp.dot(signal[:rows], weights, preferred_element_type=jnp.float32)
        if lag == 0:
            total[...] = part
        else:
            total[lag * group :, :] += part
    out_ref[...] = total[...].astype(jnp.bfloat16).reshape(chunks, group, width)


def local(qkv, short_w, skip, long_h):
    rows, _, channels = qkv.shape
    k_short = short_w.shape[0]
    n_ctx = lax.axis_size("ctx")
    chan = channels // n_ctx
    groups = chan // GROUP
    steps = channels // LANES
    streams = jnp.transpose(qkv, (1, 0, 2))
    weights = jnp.transpose(short_w, (1, 0, 2))
    halo = lax.ppermute(
        streams[:, rows - (k_short - 1) :, :], "ctx", [(s, s + 1) for s in range(n_ctx - 1)]
    )
    halo_spec = pl.BlockSpec((3, k_short - 1, LANES), lambda i: (0, 0, i))
    taps_spec = pl.BlockSpec((3, k_short, LANES), lambda i: (0, 0, i))
    token_spec = pl.BlockSpec((rows, LANES), lambda i: (0, i))
    turned_spec = pl.BlockSpec((LANES, rows), lambda i: (i, 0))
    gated, turned = pl.pallas_call(
        gate_kernel,
        grid=(steps,),
        in_specs=[
            pl.BlockSpec((pl.Element(2), pl.Element(rows), pl.Element(LANES)), lambda i: (1, 0, i * LANES)),
            halo_spec,
            taps_spec,
        ],
        out_specs=[token_spec, turned_spec],
        out_shape=[
            jax.ShapeDtypeStruct((rows, channels), jnp.bfloat16),
            jax.ShapeDtypeStruct((channels, rows), jnp.bfloat16),
        ],
        scratch_shapes=[pltpu.VMEM((rows + 8, LANES), jnp.float32)] * 2,
        name="gate",
    )(streams, halo, weights)
    columns = lax.all_to_all(turned.reshape(n_ctx, chan, rows), "ctx", 0, 0, tiled=True)
    own = lax.dynamic_index_in_dim(long_h, lax.axis_index("fft"), 0, False)
    taps = jnp.pad(own.reshape(groups, 1, -1), ((0, 0), (0, 0), (2 * SUB, 0)))
    span = taps.shape[-1]
    longconv = pl.pallas_call(
        conv_kernel,
        grid=(groups,),
        in_specs=[
            pl.BlockSpec((n_ctx, GROUP, rows), lambda g: (0, g, 0)),
            pl.BlockSpec((1, 1, span), lambda g: (g, 0, 0)),
        ],
        out_specs=pl.BlockSpec((n_ctx, GROUP, rows), lambda g: (0, g, 0)),
        out_shape=jax.ShapeDtypeStruct((n_ctx, chan, rows), jnp.bfloat16),
        scratch_shapes=[
            pltpu.VMEM((SUB, span - SUB), jnp.bfloat16),
            pltpu.VMEM((n_ctx * GROUP, rows), jnp.float32),
        ],
        name="longconv",
    )(columns, taps)
    back = lax.all_to_all(longconv, "ctx", 0, 0, tiled=True).reshape(channels, rows)
    return pl.pallas_call(
        finish_kernel,
        grid=(steps,),
        in_specs=[
            pl.BlockSpec((1, rows, LANES), lambda i: (0, 0, i)),
            halo_spec,
            taps_spec,
            pl.BlockSpec((1, LANES), lambda i: (0, i)),
            token_spec,
            turned_spec,
        ],
        out_specs=token_spec,
        out_shape=jax.ShapeDtypeStruct((rows, channels), jnp.bfloat16),
        scratch_shapes=[pltpu.VMEM((rows + 8, LANES), jnp.float32)],
        name="finish",
    )(streams, halo, weights, skip.reshape(1, channels), gated, back)


def solution(mesh):
    in_specs = (P("ctx", None, "fft"), P(None, None, "fft"), P("fft"), P(None, "ctx", None, None))
    out_specs = P("ctx", "fft")
    return jax.shard_map(local, mesh=mesh, in_specs=in_specs, out_specs=out_specs, check_vma=False)
```

```python
import jax
import jax.numpy as jnp
from jax import lax
from jax.experimental import pallas as pl
from jax.experimental.pallas import tpu as pltpu
from jax.sharding import PartitionSpec as P

GROUP = 16
LANES = 256
TILE = 256
SUB = 128
MIB = 1 << 20


def depthwise(rows_ref, halo, taps, scratch):
    rows = rows_ref.shape[0]
    scratch[8:, :] = rows_ref[...].astype(jnp.float32)
    scratch[8 - halo.shape[0] : 8, :] = halo
    total = taps[0] * scratch[8 : 8 + rows, :]
    for offset in range(1, len(taps)):
        total = total + taps[offset] * scratch[8 - offset : 8 - offset + rows, :]
    return total


def stream_taps(taps_ref, stream):
    return [taps_ref[j, stream : stream + 1, :].astype(jnp.float32) for j in range(taps_ref.shape[0])]


def gate_of(keys_ref, values_ref, halo_ref, taps_ref, scratch):
    halo = halo_ref[...].astype(jnp.float32)
    feat_one = depthwise(keys_ref, halo[1], stream_taps(taps_ref, 1), scratch.at[0])
    feat_two = depthwise(values_ref, halo[2], stream_taps(taps_ref, 2), scratch.at[1])
    return (feat_one * feat_two).astype(jnp.bfloat16)


def gate_kernel(streams_ref, halo_ref, taps_ref, turned_ref, scratch):
    gated = gate_of(streams_ref.at[0], streams_ref.at[1], halo_ref, taps_ref, scratch)
    turned_ref[...] = gated.T


def prepare_kernel(streams_ref, halo_ref, taps_ref, gated_ref, scratch):
    at = pl.ds(pl.multiple_of(pl.program_id(0) * LANES, LANES), LANES)
    gated_ref[:, at] = gate_of(streams_ref.at[0], streams_ref.at[1], halo_ref, taps_ref, scratch)


def build(taps_ref, group, kind, table, start, size):
    window = jnp.broadcast_to(taps_ref[group, kind, :, start : start + size + SUB], (SUB, size + SUB))
    turned = pltpu.roll(window, 0, axis=1, stride=1, stride_axis=0)
    table[group, kind, :, start : start + size] = turned[:, SUB:].astype(jnp.bfloat16)


def conv_kernel(signal_ref, taps_ref, out_ref, table, summed, held):
    chunks, chan, width = signal_ref.shape
    groups = chan // GROUP
    columns = table.shape[-1]
    pad = 2 * TILE - SUB

    for g in range(groups):
        rows = slice(g * GROUP, (g + 1) * GROUP)
        even = signal_ref[:, rows, :TILE].astype(jnp.float32)
        odd = signal_ref[:, rows, TILE:].astype(jnp.float32)
        summed[g] = (even + odd).astype(jnp.bfloat16)

    def left(g, product, chunk):
        if product == 2:
            return summed[g, chunk]
        return signal_ref[chunk, g * GROUP : (g + 1) * GROUP, product * TILE : (product + 1) * TILE]

    def factor(g, product, lag):
        at = pad + lag * width + (TILE if product == 1 else 0)
        kind = 1 if product == 2 else 0
        return jnp.concatenate(
            [table[g, kind, :, at - k * SUB : at - k * SUB + TILE] for k in range(TILE // SUB)], axis=0
        )

    def body(*sums):
        def total(g, product, chunk):
            return sums[(g * 2 + product % 2) * chunks + chunk]

        order = [(product, lag) for product in (2, 1, 0) for lag in range(chunks)]
        done = [0, 0]

        def stage(step):
            product, lag = order[step]
            kind = 1 if product == 2 else 0
            while done[kind] < min(pad + lag * width + 2 * TILE, columns):
                size = min(width, columns - done[kind])
                for g in range(groups):
                    build(taps_ref, g, kind, table, done[kind], size)
                done[kind] += size
            for g in range(groups):
                pltpu.matmul_push_rhs(factor(g, product, lag), step % 2, g)

        stage(0)
        last = [None] * groups
        for step, (product, lag) in enumerate(order):
            if step + 1 < len(order):
                stage(step + 1)
            for chunk in range(lag, chunks):
                for g in range(groups):
                    pltpu.matmul_acc_lhs(
                        total(g, product, chunk),
                        left(g, product, chunk - lag),
                        step % 2 if chunk == lag else None,
                    )
            for g in range(groups):
                rows = slice(g * GROUP, (g + 1) * GROUP)
                part = pltpu.matmul_pop(total(g, product, lag))
                if product == 2:
                    held[g, 0, lag] = part
                elif product == 1:
                    held[g, 0, lag] = held[g, 0, lag] - part
                    held[g, 1, lag] = part
                else:
                    even = part if lag == 0 else part + held[g, 1, lag - 1]
                    out_ref[lag, rows, :TILE] = even.astype(jnp.bfloat16)
                    out_ref[lag, rows, TILE:] = (held[g, 0, lag] - part).astype(jnp.bfloat16)

    pl.run_scoped(
        body,
        *[pltpu.ACC(g)((GROUP, TILE), jnp.float32) for g in range(groups) for _ in range(2 * chunks)],
    )


def finish_kernel(stream_ref, halo_ref, taps_ref, skip_ref, gated_ref, back_ref, out_ref, scratch):
    at = pl.ds(pl.multiple_of(pl.program_id(0) * LANES, LANES), LANES)
    halo = halo_ref[0].astype(jnp.float32)
    query = depthwise(stream_ref.at[0], halo, stream_taps(taps_ref, 0), scratch.at[0])
    inner = back_ref[at, :].T.astype(jnp.float32) + skip_ref[...] * gated_ref[:, at].astype(jnp.float32)
    out_ref[...] = (query * inner).astype(jnp.bfloat16)


def local(qkv, short_w, skip, long_h):
    rows, _, channels = qkv.shape
    k_short = short_w.shape[0]
    n_ctx = lax.axis_size("ctx")
    chan = channels // n_ctx
    groups = chan // GROUP
    steps = channels // LANES
    span = long_h.shape[-1]
    streams = jnp.transpose(qkv, (1, 0, 2))
    held = pltpu.with_memory_space_constraint(streams, pltpu.HBM)
    weights = pltpu.with_memory_space_constraint(short_w, pltpu.HBM)
    small = pltpu.CompilerParams(vmem_limit_bytes=40 * MIB)
    halo = lax.ppermute(
        streams[:, rows - (k_short - 1) :, :], "ctx", [(s, s + 1) for s in range(n_ctx - 1)]
    )
    halo_spec = pl.BlockSpec((3, k_short - 1, LANES), lambda i: (0, 0, i))
    taps_spec = pl.BlockSpec((k_short, 3, LANES), lambda i: (0, 0, i))
    pair_spec = pl.BlockSpec((pl.Element(2), pl.Element(rows), pl.Element(LANES)), lambda i: (1, 0, i * LANES))
    token_spec = pl.BlockSpec((rows, LANES), lambda i: (0, i))
    turned_spec = pl.BlockSpec((LANES, rows), lambda i: (i, 0))
    scratch = pltpu.VMEM((2, rows + 8, LANES), jnp.float32)
    turned = pl.pallas_call(
        gate_kernel,
        grid=(steps,),
        in_specs=[
            pair_spec,
            halo_spec,
            taps_spec,
        ],
        out_specs=turned_spec,
        out_shape=jax.ShapeDtypeStruct((channels, rows), jnp.bfloat16),
        scratch_shapes=[scratch],
        compiler_params=small,
        name="gate",
    )(held, halo, weights)
    columns = lax.all_to_all(turned.reshape(n_ctx, chan, rows), "ctx", 0, 0, tiled=True)
    own = lax.dynamic_index_in_dim(long_h, lax.axis_index("fft"), 0, False).reshape(groups, 1, span)
    near = jnp.pad(own, ((0, 0), (0, 0), (2 * TILE, 0)))
    both = near + jnp.pad(near[:, :, TILE:], ((0, 0), (0, 0), (0, TILE)))
    taps = jnp.stack([near, both], axis=1)
    whole = pl.BlockSpec(memory_space=pltpu.VMEM)
    gated = pl.pallas_call(
        prepare_kernel,
        grid=(steps,),
        in_specs=[pair_spec, halo_spec, taps_spec],
        out_specs=whole,
        out_shape=pltpu.VMEM((rows, channels), jnp.bfloat16),
        scratch_shapes=[scratch],
        compiler_params=small,
        cost_estimate=pl.CostEstimate(flops=32 * rows * channels, bytes_accessed=8 * MIB, transcendentals=0),
        name="prepare",
    )(held, halo, weights)
    longconv = pl.pallas_call(
        conv_kernel,
        in_specs=[whole, whole],
        out_specs=whole,
        out_shape=jax.ShapeDtypeStruct((n_ctx, chan, rows), jnp.bfloat16),
        scratch_shapes=[
            pltpu.VMEM((groups, 2, SUB, span + 2 * TILE - SUB), jnp.bfloat16),
            pltpu.VMEM((groups, n_ctx, GROUP, TILE), jnp.bfloat16),
            pltpu.VMEM((groups, 2, n_ctx, GROUP, TILE), jnp.float32),
        ],
        compiler_params=small,
        name="longconv",
    )(columns, taps)
    back = lax.all_to_all(longconv, "ctx", 0, 0, tiled=True).reshape(channels, rows)
    return pl.pallas_call(
        finish_kernel,
        grid=(steps,),
        in_specs=[
            pl.BlockSpec((1, rows, LANES), lambda i: (0, 0, i)),
            halo_spec,
            taps_spec,
            pl.BlockSpec((1, LANES), lambda i: (0, i)),
            whole,
            whole,
        ],
        out_specs=token_spec,
        out_shape=jax.ShapeDtypeStruct((rows, channels), jnp.bfloat16),
        scratch_shapes=[scratch],
        compiler_params=small,
        name="finish",
    )(
        held,
        halo,
        weights,
        skip.reshape(1, channels),
        pltpu.with_memory_space_constraint(gated, pltpu.VMEM),
        back,
    )


def solution(mesh):
    in_specs = (P("ctx", None, "fft"), P(None, None, "fft"), P("fft"), P(None, "ctx", None, None))
    out_specs = P("ctx", "fft")
    return jax.shard_map(local, mesh=mesh, in_specs=in_specs, out_specs=out_specs, check_vma=False)
```

```python
import jax
import jax.numpy as jnp
from jax import lax
from jax.experimental import pallas as pl
from jax.experimental.pallas import tpu as pltpu
from jax.sharding import PartitionSpec as P

GROUP = 16
LANES = 512
TILE = 256
SUB = 256
SEND = 4
MIB = 1 << 20


def depthwise(rows_ref, halo, taps, scratch):
    rows = rows_ref.shape[0]
    scratch[8:, :] = rows_ref[...].astype(jnp.float32)
    scratch[8 - halo.shape[0] : 8, :] = halo
    total = taps[0] * scratch[8 : 8 + rows, :]
    for offset in range(1, len(taps)):
        total = total + taps[offset] * scratch[8 - offset : 8 - offset + rows, :]
    return total


def stream_taps(taps_ref, stream):
    return [taps_ref[j, stream : stream + 1, :].astype(jnp.float32) for j in range(taps_ref.shape[0])]


def gate_of(keys_ref, values_ref, halo_ref, taps_ref, scratch):
    halo = halo_ref[...].astype(jnp.float32)
    feat_one = depthwise(keys_ref, halo[1], stream_taps(taps_ref, 1), scratch.at[0])
    feat_two = depthwise(values_ref, halo[2], stream_taps(taps_ref, 2), scratch.at[1])
    return (feat_one * feat_two).astype(jnp.bfloat16)


def depthwise_split(rows_ref, halo, taps, scratch):
    rows = rows_ref.shape[0]
    scratch[8:, :] = rows_ref[...].astype(jnp.float32)
    scratch[8 - halo.shape[0] : 8, :] = halo
    views = [scratch[pl.ds(8 - j, rows // 2, stride=2), :] for j in range(-1, len(taps))]
    return [sum(taps[j] * views[j + 1 - odd] for j in range(len(taps))) for odd in (0, 1)]


def gate_kernel(streams_ref, halo_ref, taps_ref, turned_ref, scratch):
    rows = streams_ref.shape[1]
    halo = halo_ref[...].astype(jnp.float32)
    for slab in range(LANES // 128):
        at = slice(slab * 128, (slab + 1) * 128)
        parts = [
            depthwise_split(
                streams_ref.at[k, :, at],
                halo[k + 1, :, at],
                [tap[:, at] for tap in stream_taps(taps_ref, k + 1)],
                scratch.at[slab, k],
            )
            for k in range(2)
        ]
        for odd in (0, 1):
            scratch[slab, 2, pl.ds(odd, rows // 2, stride=2), :] = parts[0][odd] * parts[1][odd]
        turned_ref[at, :] = scratch[slab, 2, :rows, :].astype(jnp.bfloat16).T


def prepare_kernel(streams_ref, halo_ref, taps_ref, query_ref, gated_ref, scratch):
    at = pl.ds(pl.multiple_of(pl.program_id(0) * LANES, LANES), LANES)
    halo = halo_ref[0].astype(jnp.float32)
    query_ref[:, at] = depthwise(streams_ref.at[0], halo, stream_taps(taps_ref, 0), scratch.at[0])
    gated_ref[...] = gate_of(streams_ref.at[1], streams_ref.at[2], halo_ref, taps_ref, scratch)


def filter_kernel(own_ref, taps_ref, out_ref):
    span = taps_ref.shape[-1]
    for g in range(taps_ref.shape[1]):
        taps = taps_ref[0, g : g + 1, :]
        out_ref[g, 0, :, : 2 * TILE] = jnp.zeros((1, 2 * TILE), jnp.float32)
        out_ref[g, 0, :, 2 * TILE :] = taps
        out_ref[g, 1, :, :TILE] = jnp.zeros((1, TILE), jnp.float32)
        out_ref[g, 1, :, TILE : 2 * TILE] = taps[:, :TILE]
        out_ref[g, 1, :, 2 * TILE : span + TILE] = taps[:, : span - TILE] + taps[:, TILE:]
        out_ref[g, 1, :, span + TILE :] = taps[:, span - TILE :]


def build(taps_ref, group, kind, table, start, size):
    window = jnp.broadcast_to(taps_ref[group, kind, :, start : start + size + SUB], (SUB, size + SUB))
    turned = pltpu.roll(window, 0, axis=1, stride=1, stride_axis=0)
    table[group, kind, :, start : start + size] = turned[:, SUB:].astype(jnp.bfloat16)


def conv_kernel(signal_ref, taps_ref, out_hbm, table, summed, held, out_ref, sent):
    chunks, chan, width = signal_ref.shape
    groups = chan // GROUP
    columns = table.shape[-1]
    pad = 2 * TILE - SUB

    for g in range(groups):
        rows = slice(g * GROUP, (g + 1) * GROUP)
        even = signal_ref[:, rows, :TILE].astype(jnp.float32)
        odd = signal_ref[:, rows, TILE:].astype(jnp.float32)
        summed[g] = (even + odd).astype(jnp.bfloat16)

    def left(g, product, chunk):
        if product == 2:
            return summed[g, chunk]
        return signal_ref[chunk, g * GROUP : (g + 1) * GROUP, product * TILE : (product + 1) * TILE]

    def factor(g, product, lag):
        at = pad + lag * width + (TILE if product == 1 else 0)
        kind = 1 if product == 2 else 0
        return jnp.concatenate(
            [table[g, kind, :, at - k * SUB : at - k * SUB + TILE] for k in range(TILE // SUB)], axis=0
        )

    def send(piece):
        at = pl.ds(piece * SEND, SEND)
        return pltpu.make_async_copy(out_ref.at[at], out_hbm.at[at], sent.at[piece])

    def body(*sums):
        def total(g, product, chunk):
            return sums[(g * 2 + product % 2) * chunks + chunk]

        order = [(product, lag) for product in (2, 1, 0) for lag in range(chunks)]
        done = [0, 0]

        def stage(step):
            product, lag = order[step]
            kind = 1 if product == 2 else 0
            while done[kind] < min(pad + lag * width + 2 * TILE, columns):
                size = min(width, columns - done[kind])
                for g in range(groups):
                    build(taps_ref, g, kind, table, done[kind], size)
                done[kind] += size
            for g in range(groups):
                pltpu.matmul_push_rhs(factor(g, product, lag), step % 2, g)

        stage(0)
        for step, (product, lag) in enumerate(order):
            if step + 1 < len(order):
                stage(step + 1)
            for chunk in range(lag, chunks):
                for g in range(groups):
                    pltpu.matmul_acc_lhs(
                        total(g, product, chunk),
                        left(g, product, chunk - lag),
                        step % 2 if chunk == lag else None,
                    )
            for g in range(groups):
                rows = slice(g * GROUP, (g + 1) * GROUP)
                part = pltpu.matmul_pop(total(g, product, lag))
                if product == 2:
                    held[g, 0, lag] = part
                elif product == 1:
                    held[g, 0, lag] = held[g, 0, lag] - part
                    held[g, 1, lag] = part
                else:
                    even = part if lag == 0 else part + held[g, 1, lag - 1]
                    out_ref[lag, rows, :TILE] = even.astype(jnp.bfloat16)
                    out_ref[lag, rows, TILE:] = (held[g, 0, lag] - part).astype(jnp.bfloat16)
            if product == 0 and (lag + 1) % SEND == 0:
                send(lag // SEND).start()

    pl.run_scoped(
        body,
        *[pltpu.ACC(g)((GROUP, TILE), jnp.float32) for g in range(groups) for _ in range(2 * chunks)],
    )
    for piece in range(chunks // SEND):
        send(piece).wait()


def finish_kernel(query_ref, skip_ref, gated_ref, back_ref, out_ref):
    at = pl.ds(pl.multiple_of(pl.program_id(0) * LANES, LANES), LANES)
    inner = back_ref[at, :].T.astype(jnp.float32) + skip_ref[...] * gated_ref[...].astype(jnp.float32)
    out_ref[...] = (query_ref[:, at] * inner).astype(jnp.bfloat16)


def local(qkv, short_w, skip, long_h):
    rows, _, channels = qkv.shape
    k_short = short_w.shape[0]
    n_ctx = lax.axis_size("ctx")
    chan = channels // n_ctx
    groups = chan // GROUP
    steps = channels // LANES
    span = long_h.shape[-1]
    streams = jnp.transpose(qkv, (1, 0, 2))
    held = pltpu.with_memory_space_constraint(streams, pltpu.HBM)
    weights = pltpu.with_memory_space_constraint(short_w, pltpu.HBM)
    small = pltpu.CompilerParams(vmem_limit_bytes=40 * MIB)
    halo = lax.ppermute(
        streams[:, rows - (k_short - 1) :, :], "ctx", [(s, s + 1) for s in range(n_ctx - 1)]
    )
    halo_spec = pl.BlockSpec((3, k_short - 1, LANES), lambda i: (0, 0, i))
    taps_spec = pl.BlockSpec((k_short, 3, LANES), lambda i: (0, 0, i))
    pair_spec = pl.BlockSpec((pl.Element(2), pl.Element(rows), pl.Element(LANES)), lambda i: (1, 0, i * LANES))
    token_spec = pl.BlockSpec((rows, LANES), lambda i: (0, i))
    turned_spec = pl.BlockSpec((LANES, rows), lambda i: (i, 0))
    scratch = pltpu.VMEM((2, rows + 8, LANES), jnp.float32)
    turned = pl.pallas_call(
        gate_kernel,
        grid=(steps,),
        in_specs=[
            pair_spec,
            halo_spec,
            taps_spec,
        ],
        out_specs=turned_spec,
        out_shape=jax.ShapeDtypeStruct((channels, rows), jnp.bfloat16),
        scratch_shapes=[pltpu.VMEM((LANES // 128, 3, rows + 8, 128), jnp.float32)],
        compiler_params=small,
        name="gate",
    )(held, halo, weights)
    columns = lax.all_to_all(turned.reshape(n_ctx, chan, rows), "ctx", 0, 0, tiled=True)
    filters = pltpu.with_memory_space_constraint(long_h.reshape(-1, groups, span), pltpu.HBM)
    taps = pl.pallas_call(
        filter_kernel,
        grid_spec=pltpu.PrefetchScalarGridSpec(
            num_scalar_prefetch=1,
            grid=(1,),
            in_specs=[pl.BlockSpec((1, groups, span), lambda i, own: (own[0], 0, 0))],
            out_specs=pl.BlockSpec((groups, 2, 1, span + 2 * TILE), lambda i, own: (0, 0, 0, 0)),
        ),
        out_shape=jax.ShapeDtypeStruct((groups, 2, 1, span + 2 * TILE), jnp.float32),
        compiler_params=small,
        cost_estimate=pl.CostEstimate(flops=8 * span, bytes_accessed=2 * MIB, transcendentals=0),
        name="filter",
    )(lax.axis_index("fft").reshape(1), filters)
    whole = pl.BlockSpec(memory_space=pltpu.VMEM)
    query, gated = pl.pallas_call(
        prepare_kernel,
        grid=(steps,),
        in_specs=[pl.BlockSpec((3, rows, LANES), lambda i: (0, 0, i)), halo_spec, taps_spec],
        out_specs=[whole, token_spec],
        out_shape=[pltpu.VMEM((rows, channels), jnp.float32), pltpu.HBM((rows, channels), jnp.bfloat16)],
        scratch_shapes=[scratch],
        compiler_params=small,
        cost_estimate=pl.CostEstimate(flops=32 * rows * channels, bytes_accessed=8 * MIB, transcendentals=0),
        name="prepare",
    )(held, halo, weights)
    longconv = pl.pallas_call(
        conv_kernel,
        in_specs=[whole, whole],
        out_specs=pl.BlockSpec(memory_space=pltpu.HBM),
        out_shape=pltpu.HBM((n_ctx, chan, rows), jnp.bfloat16),
        scratch_shapes=[
            pltpu.VMEM((groups, 2, SUB, span + 2 * TILE - SUB), jnp.bfloat16),
            pltpu.VMEM((groups, n_ctx, GROUP, TILE), jnp.bfloat16),
            pltpu.VMEM((groups, 2, n_ctx, GROUP, TILE), jnp.float32),
            pltpu.VMEM((n_ctx, chan, rows), jnp.bfloat16),
            pltpu.SemaphoreType.DMA((n_ctx // SEND,)),
        ],
        compiler_params=small,
        name="longconv",
    )(columns, taps)
    back = lax.all_to_all(longconv, "ctx", 0, 0, tiled=True).reshape(channels, rows)
    return pl.pallas_call(
        finish_kernel,
        grid=(steps,),
        in_specs=[whole, pl.BlockSpec((1, LANES), lambda i: (0, i)), token_spec, whole],
        out_specs=token_spec,
        out_shape=jax.ShapeDtypeStruct((rows, channels), jnp.bfloat16),
        compiler_params=small,
        name="finish",
    )(
        pltpu.with_memory_space_constraint(query, pltpu.VMEM),
        skip.reshape(1, channels),
        pltpu.with_memory_space_constraint(gated, pltpu.HBM),
        back,
    )


def solution(mesh):
    in_specs = (P("ctx", None, "fft"), P(None, None, "fft"), P("fft"), P(None, "ctx", None, None))
    out_specs = P("ctx", "fft")
    return jax.shard_map(local, mesh=mesh, in_specs=in_specs, out_specs=out_specs, check_vma=False)
```

```python
import jax
import jax.numpy as jnp
from jax import lax
from jax.experimental import pallas as pl
from jax.experimental.pallas import tpu as pltpu
from jax.sharding import PartitionSpec as P

GROUP = 16
LANES = 512
TILE = 256
SUB = 128
SPREAD = 4
DELAY = 2
SEND = 4
MIB = 1 << 20


def depthwise(rows_ref, halo, taps, scratch):
    rows = rows_ref.shape[0]
    scratch[8:, :] = rows_ref[...].astype(jnp.float32)
    scratch[8 - halo.shape[0] : 8, :] = halo
    total = taps[0] * scratch[8 : 8 + rows, :]
    for offset in range(1, len(taps)):
        total = total + taps[offset] * scratch[8 - offset : 8 - offset + rows, :]
    return total


def stream_taps(taps_ref, stream):
    return [taps_ref[j, stream : stream + 1, :].astype(jnp.float32) for j in range(taps_ref.shape[0])]


def gate_of(keys_ref, values_ref, halo_ref, taps_ref, scratch):
    halo = halo_ref[...].astype(jnp.float32)
    feat_one = depthwise(keys_ref, halo[1], stream_taps(taps_ref, 1), scratch.at[0])
    feat_two = depthwise(values_ref, halo[2], stream_taps(taps_ref, 2), scratch.at[1])
    return (feat_one * feat_two).astype(jnp.bfloat16)


def depthwise_split(rows_ref, halo, taps, scratch):
    rows = rows_ref.shape[0]
    scratch[8:, :] = rows_ref[...].astype(jnp.float32)
    scratch[8 - halo.shape[0] : 8, :] = halo
    views = [scratch[pl.ds(8 - j, rows // 2, stride=2), :] for j in range(-1, len(taps))]
    return [sum(taps[j] * views[j + 1 - odd] for j in range(len(taps))) for odd in (0, 1)]


def gate_kernel(streams_ref, halo_ref, taps_ref, turned_ref, scratch):
    rows = streams_ref.shape[1]
    halo = halo_ref[...].astype(jnp.float32)
    for slab in range(LANES // 128):
        at = slice(slab * 128, (slab + 1) * 128)
        parts = [
            depthwise_split(
                streams_ref.at[k, :, at],
                halo[k + 1, :, at],
                [tap[:, at] for tap in stream_taps(taps_ref, k + 1)],
                scratch.at[slab, k],
            )
            for k in range(2)
        ]
        for odd in (0, 1):
            scratch[slab, 2, pl.ds(odd, rows // 2, stride=2), :] = parts[0][odd] * parts[1][odd]
        turned_ref[at, :] = scratch[slab, 2, :rows, :].astype(jnp.bfloat16).T


def prepare_kernel(streams_ref, halo_ref, taps_ref, query_ref, gated_ref, scratch):
    at = pl.ds(pl.multiple_of(pl.program_id(0) * LANES, LANES), LANES)
    halo = halo_ref[0].astype(jnp.float32)
    query_ref[:, at] = depthwise(streams_ref.at[0], halo, stream_taps(taps_ref, 0), scratch.at[0])
    gated_ref[...] = gate_of(streams_ref.at[1], streams_ref.at[2], halo_ref, taps_ref, scratch)


def filter_kernel(own_ref, taps_ref, out_ref):
    span = taps_ref.shape[-1]
    for g in range(taps_ref.shape[1]):
        taps = taps_ref[0, g : g + 1, :]
        out_ref[g, 0, :, : 2 * TILE] = jnp.zeros((1, 2 * TILE), jnp.float32)
        out_ref[g, 0, :, 2 * TILE :] = taps
        out_ref[g, 1, :, :TILE] = jnp.zeros((1, TILE), jnp.float32)
        out_ref[g, 1, :, TILE : 2 * TILE] = taps[:, :TILE]
        out_ref[g, 1, :, 2 * TILE : span + TILE] = taps[:, : span - TILE] + taps[:, TILE:]
        out_ref[g, 1, :, span + TILE :] = taps[:, span - TILE :]


def build(taps_ref, group, kind, table, start, size):
    window = jnp.broadcast_to(taps_ref[group, kind, :, start : start + size + SUB], (SUB, size + SUB))
    turned = pltpu.roll(window, 0, axis=1, stride=1, stride_axis=0)
    table[group, kind, :, start : start + size] = turned[:, SUB:].astype(jnp.bfloat16)


def conv_kernel(signal_ref, taps_ref, out_hbm, table, summed, held, out_ref, sent):
    chunks, chan, width = signal_ref.shape
    groups = chan // GROUP
    columns = table.shape[-1]
    pad = 2 * TILE - SUB

    for g in range(groups):
        rows = slice(g * GROUP, (g + 1) * GROUP)
        even = signal_ref[:, rows, :TILE].astype(jnp.float32)
        odd = signal_ref[:, rows, TILE:].astype(jnp.float32)
        summed[g] = (even + odd).astype(jnp.bfloat16)

    def left(g, product, chunk):
        if product == 2:
            return summed[g, chunk]
        return signal_ref[chunk, g * GROUP : (g + 1) * GROUP, product * TILE : (product + 1) * TILE]

    def factor(g, product, lag):
        at = pad + lag * width + (TILE if product == 1 else 0)
        kind = 1 if product == 2 else 0
        return jnp.concatenate(
            [table[g, kind, :, at - k * SUB : at - k * SUB + TILE] for k in range(TILE // SUB)], axis=0
        )

    def send(piece):
        at = pl.ds(piece * SEND, SEND)
        return pltpu.make_async_copy(out_ref.at[at], out_hbm.at[at], sent.at[piece])

    def body(*sums):
        def total(g, product, chunk):
            return sums[(g * 2 + product % 2) * chunks + chunk]

        order = [(product, lag) for product in (2, 1, 0) for lag in range(chunks)]
        done = [0, 0]

        def stage(step):
            product, lag = order[step]
            kind = 1 if product == 2 else 0
            while done[kind] < min(pad + lag * width + 2 * TILE, columns):
                size = min(SPREAD * width if done[kind] else width, columns - done[kind])
                for g in range(groups):
                    build(taps_ref, g, kind, table, done[kind], size)
                done[kind] += size
            for g in range(groups):
                pltpu.matmul_push_rhs(factor(g, product, lag), step % 2, g)

        def finish(product, lag):
            for g in range(groups):
                rows = slice(g * GROUP, (g + 1) * GROUP)
                part = pltpu.matmul_pop(total(g, product, lag))
                if product == 2:
                    held[g, 0, lag] = part
                elif product == 1:
                    held[g, 0, lag] = held[g, 0, lag] - part
                    held[g, 1, lag] = part
                else:
                    even = part if lag == 0 else part + held[g, 1, lag - 1]
                    out_ref[lag, rows, :TILE] = even.astype(jnp.bfloat16)
                    out_ref[lag, rows, TILE:] = (held[g, 0, lag] - part).astype(jnp.bfloat16)
            if product == 0 and (lag + 1) % SEND == 0:
                send(lag // SEND).start()

        stage(0)
        for step, (product, lag) in enumerate(order):
            if step + 1 < len(order):
                stage(step + 1)
            for chunk in range(lag, chunks):
                for g in range(groups):
                    pltpu.matmul_acc_lhs(
                        total(g, product, chunk),
                        left(g, product, chunk - lag),
                        step % 2 if chunk == lag else None,
                    )
            if step >= DELAY:
                finish(*order[step - DELAY])
        for step in range(len(order) - DELAY, len(order)):
            finish(*order[step])

    pl.run_scoped(
        body,
        *[pltpu.ACC(g)((GROUP, TILE), jnp.float32) for g in range(groups) for _ in range(2 * chunks)],
    )
    for piece in range(chunks // SEND):
        send(piece).wait()


def finish_kernel(query_ref, skip_ref, gated_ref, back_ref, out_ref):
    at = pl.ds(pl.multiple_of(pl.program_id(0) * LANES, LANES), LANES)
    inner = back_ref[at, :].T.astype(jnp.float32) + skip_ref[...] * gated_ref[...].astype(jnp.float32)
    out_ref[...] = (query_ref[:, at] * inner).astype(jnp.bfloat16)


def local(qkv, short_w, skip, long_h):
    rows, _, channels = qkv.shape
    k_short = short_w.shape[0]
    n_ctx = lax.axis_size("ctx")
    chan = channels // n_ctx
    groups = chan // GROUP
    steps = channels // LANES
    span = long_h.shape[-1]
    streams = jnp.transpose(qkv, (1, 0, 2))
    held = pltpu.with_memory_space_constraint(streams, pltpu.HBM)
    weights = pltpu.with_memory_space_constraint(short_w, pltpu.HBM)
    small = pltpu.CompilerParams(vmem_limit_bytes=40 * MIB)
    halo = lax.ppermute(
        streams[:, rows - (k_short - 1) :, :], "ctx", [(s, s + 1) for s in range(n_ctx - 1)]
    )
    halo_spec = pl.BlockSpec((3, k_short - 1, LANES), lambda i: (0, 0, i))
    taps_spec = pl.BlockSpec((k_short, 3, LANES), lambda i: (0, 0, i))
    pair_spec = pl.BlockSpec((pl.Element(2), pl.Element(rows), pl.Element(LANES)), lambda i: (1, 0, i * LANES))
    token_spec = pl.BlockSpec((rows, LANES), lambda i: (0, i))
    turned_spec = pl.BlockSpec((LANES, rows), lambda i: (i, 0))
    scratch = pltpu.VMEM((2, rows + 8, LANES), jnp.float32)
    turned = pl.pallas_call(
        gate_kernel,
        grid=(steps,),
        in_specs=[
            pair_spec,
            halo_spec,
            taps_spec,
        ],
        out_specs=turned_spec,
        out_shape=jax.ShapeDtypeStruct((channels, rows), jnp.bfloat16),
        scratch_shapes=[pltpu.VMEM((LANES // 128, 3, rows + 8, 128), jnp.float32)],
        compiler_params=small,
        name="gate",
    )(held, halo, weights)
    columns = lax.all_to_all(turned.reshape(n_ctx, chan, rows), "ctx", 0, 0, tiled=True)
    filters = pltpu.with_memory_space_constraint(long_h.reshape(-1, groups, span), pltpu.HBM)
    taps = pl.pallas_call(
        filter_kernel,
        grid_spec=pltpu.PrefetchScalarGridSpec(
            num_scalar_prefetch=1,
            grid=(1,),
            in_specs=[pl.BlockSpec((1, groups, span), lambda i, own: (own[0], 0, 0))],
            out_specs=pl.BlockSpec((groups, 2, 1, span + 2 * TILE), lambda i, own: (0, 0, 0, 0)),
        ),
        out_shape=jax.ShapeDtypeStruct((groups, 2, 1, span + 2 * TILE), jnp.float32),
        compiler_params=small,
        cost_estimate=pl.CostEstimate(flops=8 * span, bytes_accessed=2 * MIB, transcendentals=0),
        name="filter",
    )(lax.axis_index("fft").reshape(1), filters)
    whole = pl.BlockSpec(memory_space=pltpu.VMEM)
    query, gated = pl.pallas_call(
        prepare_kernel,
        grid=(steps,),
        in_specs=[pl.BlockSpec((3, rows, LANES), lambda i: (0, 0, i)), halo_spec, taps_spec],
        out_specs=[whole, token_spec],
        out_shape=[pltpu.VMEM((rows, channels), jnp.float32), pltpu.HBM((rows, channels), jnp.bfloat16)],
        scratch_shapes=[scratch],
        compiler_params=small,
        cost_estimate=pl.CostEstimate(flops=32 * rows * channels, bytes_accessed=8 * MIB, transcendentals=0),
        name="prepare",
    )(held, halo, weights)
    longconv = pl.pallas_call(
        conv_kernel,
        in_specs=[whole, whole],
        out_specs=pl.BlockSpec(memory_space=pltpu.HBM),
        out_shape=pltpu.HBM((n_ctx, chan, rows), jnp.bfloat16),
        scratch_shapes=[
            pltpu.VMEM((groups, 2, SUB, span + 2 * TILE - SUB), jnp.bfloat16),
            pltpu.VMEM((groups, n_ctx, GROUP, TILE), jnp.bfloat16),
            pltpu.VMEM((groups, 2, n_ctx, GROUP, TILE), jnp.float32),
            pltpu.VMEM((n_ctx, chan, rows), jnp.bfloat16),
            pltpu.SemaphoreType.DMA((n_ctx // SEND,)),
        ],
        compiler_params=small,
        name="longconv",
    )(columns, taps)
    back = lax.all_to_all(longconv, "ctx", 0, 0, tiled=True).reshape(channels, rows)
    return pl.pallas_call(
        finish_kernel,
        grid=(steps,),
        in_specs=[whole, pl.BlockSpec((1, LANES), lambda i: (0, i)), token_spec, whole],
        out_specs=token_spec,
        out_shape=jax.ShapeDtypeStruct((rows, channels), jnp.bfloat16),
        compiler_params=small,
        name="finish",
    )(
        pltpu.with_memory_space_constraint(query, pltpu.VMEM),
        skip.reshape(1, channels),
        pltpu.with_memory_space_constraint(gated, pltpu.HBM),
        back,
    )


def solution(mesh):
    in_specs = (P("ctx", None, "fft"), P(None, None, "fft"), P("fft"), P(None, "ctx", None, None))
    out_specs = P("ctx", "fft")
    return jax.shard_map(local, mesh=mesh, in_specs=in_specs, out_specs=out_specs, check_vma=False)
```
